256 devices in a mesh: seq: 16 (over z, core), tensor: 16 (over x, y).
Axes of the slice: x: 4, y: 4, z: 8, core: 2. Of those that a mesh axis runs over, the one named last changes fastest.
Arguments:
- tokens: bfloat16 [4096, 7168], P('seq', 'tensor')
- positions: int32 [4096], P('seq'), may hold values from 0 to 4095, as said below
- w_down_q: bfloat16 [7168, 1536], P('tensor')
- w_down_kv: bfloat16 [7168, 512], P('tensor')
- w_rope_key: bfloat16 [7168, 64], P('tensor'), may hold values from -0.0625 to 0.0625
- gain_query: float32 [1536], replicated, may hold values from 0.25 to 1.75
- gain_kv: float32 [512], replicated, may hold values from 0.25 to 1.75
- w_up_q: bfloat16 [1536, 12288], P(None, 'tensor')
- w_up_kv: bfloat16 [512, 16384], P(None, 'tensor')
Outputs:
- attended: bfloat16 [4096, 8192], P('seq', 'tensor')
The draws below stay inside these ranges and needn't reach their ends.
Inputs may be any that keep to these rules, and one draw needn't show every extreme that they name: The positions of the window's 4096 tokens are 0 to 4095, each once, in runs of 16 consecutive values that start at multiples of 16.
All inputs are finite; a program needn't handle non-finite values.
Results may differ from the reference program's by a relative error of at most 0.012.
The reference program's roundings to bfloat16 on the way count: a program that leaves them out, or rounds other values in their place, can miss the bound.
Values may be sent and summed in bfloat16 or wider, within the bound.
A program may use at most 128 MiB of HBM per device.

```python
import jax
import jax.numpy as jnp
from jax import lax

D = 7168
QL = 1536
KVL = 512
NOPE = 128
ROPE = 64
VDIM = 128
HEADS = 64
TOKENS = 4096
PBLK = 16
N_TENSOR = 16


def column_ramp(count, power):
    spot = jnp.arange(count, dtype=jnp.float32) / max(count - 1, 1)
    return 10.0 ** (power * spot)


def spiked(key, rows, cols, power):
    noise_key, pair_key = jax.random.split(key)
    base = jax.random.normal(noise_key, (rows, cols), jnp.float32) / jnp.sqrt(jnp.float32(D))
    pairing = jax.random.permutation(pair_key, N_TENSOR)
    row_block = jnp.arange(rows) // (rows // N_TENSOR)
    col_block = jnp.arange(cols) // (cols // N_TENSOR)
    struck = pairing[row_block][:, None] == col_block[None, :]
    return base * jnp.where(struck, 3.0, 1.0) * column_ramp(cols, power)[None, :]


def latent_kv_rows(key, power):
    return spiked(jax.random.fold_in(key, 11), D, KVL, power)


def up_kv_rows(key):
    return jax.random.normal(jax.random.fold_in(key, 23), (KVL, HEADS * (NOPE + VDIM)), jnp.float32) / jnp.sqrt(jnp.float32(KVL))


def draw_w_down_kv(key, part):
    power = 0.5
    return latent_kv_rows(key, power).astype(jnp.bfloat16)


def draw_w_down_q(key, part):
    power = 0.5
    whole = spiked(jax.random.fold_in(key, 5), D, QL, power)
    return whole.astype(jnp.bfloat16)


def draw_w_up_kv(key, part):
    return up_kv_rows(key).astype(jnp.bfloat16)


def draw_w_up_q(key, part):
    base = jax.random.normal(jax.random.fold_in(key, 29), (QL, HEADS * (NOPE + ROPE)), jnp.float32) / jnp.sqrt(jnp.float32(QL))
    return base.astype(jnp.bfloat16)


def draw_tokens(key, part):
    noise_key, scale_key = jax.random.split(key, 2)
    noise = jax.random.normal(noise_key, (TOKENS, D), jnp.float32)
    row_scale = jnp.exp(jax.random.uniform(scale_key, (TOKENS,), jnp.float32, 0.0, jnp.log(10.0)))
    whole = noise * row_scale[:, None]
    return whole.astype(jnp.bfloat16)


def draw_positions(key, part):
    order = jax.random.permutation(key, TOKENS // PBLK)
    runs = order[:, None] * PBLK + jnp.arange(PBLK)[None, :]
    return runs.reshape(TOKENS).astype(jnp.int32)


def block_levels(key, shape, shards, low, high):
    def one(position, shards_of):
        draws = jax.random.uniform(jax.random.fold_in(jax.random.fold_in(key, 6), position), (shards_of,), jnp.float32, low / len(shards), high / len(shards))
        return jnp.repeat(jnp.exp(draws), shape[position] // shards_of).reshape((-1,) + (1,) * (len(shape) - position - 1))

    factor_of = one(*shards[0])
    for cut in shards[1:]:
        factor_of = factor_of * one(*cut)
    return factor_of


def gaussian(stream_key, dims, scale, bound, cuts=(), held_as=jnp.bfloat16):
    result = jax.random.normal(stream_key, dims, jnp.float32) * scale
    if len(cuts) > 0:
        result = block_levels(stream_key, dims, cuts, -0.22, 0.18) * result
    return jnp.clip(result, min=-bound, max=bound).astype(held_as)


def setup_inputs(seed: int = 0) -> dict:
    seeds = jax.random.split(jax.random.key(seed), 10)
    return {
        "tokens": draw_tokens(jax.random.fold_in(seeds[9], 71), 0),
        "positions": draw_positions(jax.random.fold_in(seeds[9], 71), 0),
        "w_down_q": draw_w_down_q(jax.random.fold_in(seeds[9], 71), 0),
        "w_down_kv": draw_w_down_kv(jax.random.fold_in(seeds[9], 71), 0),
        "w_rope_key": gaussian(seeds[4], (D, ROPE), D ** -0.5, 0.0625, ((0, 16),)),
        "gain_query": jnp.clip(1.0 + 0.15 * jax.random.normal(seeds[5], (QL,), jnp.float32), 0.25, 1.75),
        "gain_kv": jnp.clip(1.0 + 0.15 * jax.random.normal(seeds[6], (KVL,), jnp.float32), 0.25, 1.75),
        "w_up_q": draw_w_up_q(jax.random.fold_in(seeds[9], 71), 0),
        "w_up_kv": draw_w_up_kv(jax.random.fold_in(seeds[9], 71), 0),
    }


epsilon = 1e-06

def angles(where_at, width):
    half = width // 2
    freq = 10000.0 ** (-(jnp.arange(half, dtype=jnp.float32) * 2.0 / width))
    return where_at.astype(jnp.float32)[:, None] * freq[None, :]

def rotate(vector, angle):
    half = vector.shape[-1] // 2
    first = vector[..., :half]
    second = vector[..., half:]
    cosine = jnp.cos(angle)
    sine = jnp.sin(angle)
    return jnp.concatenate([first * cosine - second * sine, second * cosine + first * sine], axis=-1)

def normed(values, gain):
    mean_sq = lax.optimization_barrier(jnp.mean(values * values, axis=-1, keepdims=True))
    return values * lax.rsqrt(mean_sq + epsilon) * gain

def reference(tokens, positions, w_down_q, w_down_kv, w_rope_key, gain_query, gain_kv, w_up_q, w_up_kv):
    softmax_scale = (1.0 + 0.1 * jnp.log(40.0)) ** 2 / jnp.sqrt(jnp.float32(NOPE + ROPE))
    down_q = jnp.dot(tokens, w_down_q, preferred_element_type=jnp.float32)
    down_kv = jnp.dot(tokens, w_down_kv, preferred_element_type=jnp.float32)
    rope_raw = jnp.dot(tokens, w_rope_key, preferred_element_type=jnp.float32)
    latent_q = normed(down_q, gain_query).astype(jnp.bfloat16)
    latent_kv = normed(down_kv, gain_kv).astype(jnp.bfloat16)
    turn = angles(positions, ROPE)
    rope_key = rotate(rope_raw, turn).astype(jnp.bfloat16)
    query = jnp.dot(latent_q, w_up_q, preferred_element_type=jnp.float32).reshape(TOKENS, HEADS, NOPE + ROPE)
    query_nope = query[..., :NOPE].astype(jnp.bfloat16)
    query_rope = rotate(query[..., NOPE:], turn[:, None, :]).astype(jnp.bfloat16)
    keyval = jnp.dot(latent_kv, w_up_kv, preferred_element_type=jnp.float32).astype(jnp.bfloat16)
    keyval = keyval.reshape(TOKENS, HEADS, NOPE + VDIM)
    key_nope = keyval[..., :NOPE]
    values = keyval[..., NOPE:]
    visible = positions[None, :] <= positions[:, None]

    def one_head(inputs):
        head_qn, head_qr, head_kn, head_val = inputs
        scores = jnp.dot(head_qn, head_kn.T, preferred_element_type=jnp.float32)
        scores = scores + jnp.dot(head_qr, rope_key.T, preferred_element_type=jnp.float32)
        scores = jnp.where(visible, scores * softmax_scale, jnp.float32(-1e+30))
        top = lax.optimization_barrier(jnp.max(scores, axis=-1, keepdims=True))
        weights = jnp.where(visible, jnp.exp(scores - top), jnp.float32(0.0))
        total = lax.optimization_barrier(jnp.sum(weights, axis=-1, keepdims=True))
        mixed = jnp.dot(weights.astype(jnp.bfloat16), head_val, preferred_element_type=jnp.float32) / total
        return mixed.astype(jnp.bfloat16)
    stacked = (jnp.moveaxis(query_nope, 1, 0), jnp.moveaxis(query_rope, 1, 0), jnp.moveaxis(key_nope, 1, 0), jnp.moveaxis(values, 1, 0))
    heads_out = lax.map(one_head, stacked)
    return jnp.moveaxis(heads_out, 0, 1).reshape(TOKENS, HEADS * VDIM)
```

```python
import functools

import numpy as np
import jax
import jax.numpy as jnp
from jax import lax
from jax.experimental import pallas as pl
from jax.experimental.pallas import tpu as pltpu
from jax.sharding import PartitionSpec as P

NOPE = 128
ROPE = 64
VDIM = 128
HEAD_DEV = 4
QL = 1536
KVL = 512
WIDE = QL + KVL + 128
LINE = KVL + 128
RUN = 16
CHUNK = 512
MESH = pl.DeviceIdType.MESH
EPS = 1e-06
F32 = jnp.float32
BF16 = jnp.bfloat16

CUTS = (((0, 640), (640, 512)), ((1152, 512), (1664, 512)))


def turned(v, cosine, sine):
    lane = lax.broadcasted_iota(jnp.int32, v.shape, 1)
    swapped = jnp.where(lane < 32, -pltpu.roll(v, 96, 1), pltpu.roll(v, 32, 1))
    return jnp.where(lane < 64, v * cosine + swapped * sine, 0.0)


def kernel(
    pos_ref, freq_ref, gq_ref, gkv_ref, tok_hbm, wq_hbm, wkv_hbm, wr_hbm, uq_hbm, ukv_hbm,
    out_ref,
    tok, wq, wkv, wr, uq, ukv,
    part, l1x, l2x, l3x, r1x, r2x, r3x, l1y, l2y, l3y, r1y, r2y, r3y,
    mid_x, mid_y, k1x, k2x, k3x, j1x, j2x, j3x, k1y, k2y, k3y, j1y, j2y, j3y,
    total, lat_q, keys, qcat, m_ref, l_ref, acc_ref,
    load_sem, send_sem, recv_sem,
):
    s = lax.axis_index("seq")
    t = lax.axis_index("tensor")
    x, y = t // 4, t % 4
    z, c = s // 2, s % 2

    loads = []
    for n, (a, b) in enumerate(
        ((tok_hbm, tok), (wq_hbm, wq), (wkv_hbm, wkv), (wr_hbm, wr), (uq_hbm, uq), (ukv_hbm, ukv))
    ):
        loads.append(pltpu.make_async_copy(a, b, load_sem.at[n]))
        loads[-1].start()

    def at(xx, yy):
        return (s, xx * 4 + yy)

    xp, xm, xo = (x + 1) % 4, (x + 3) % 4, (x + 2) % 4
    yp, ym, yo = (y + 1) % 4, (y + 3) % 4, (y + 2) % 4
    x_plus, x_minus = at(xp, y), at(xm, y)
    y_plus, y_minus = at(x, yp), at(x, ym)
    sibling = (s + 1 - 2 * c, t)
    z_peers = [(((z + d) % 8) * 2 + c, t) for d in range(1, 8)]

    barrier = pltpu.get_barrier_semaphore()
    friends = [x_plus, x_minus, y_plus, y_minus, sibling] + z_peers
    for who in friends:
        pl.semaphore_signal(barrier, inc=1, device_id=who, device_id_type=MESH)

    sent = []
    count = [0]

    def fresh(n):
        count[0] += n
        return count[0] - n

    def send(src, dst, who, k):
        copy = pltpu.make_async_remote_copy(
            src_ref=src, dst_ref=dst, send_sem=send_sem.at[k], recv_sem=recv_sem.at[k],
            device_id=who, device_id_type=MESH,
        )
        copy.start()
        sent.append(copy)

    def arrived(dst, k):
        pltpu.make_async_remote_copy(
            src_ref=dst, dst_ref=dst, send_sem=send_sem.at[k], recv_sem=recv_sem.at[k],
            device_id=sibling, device_id_type=MESH,
        ).wait_recv()

    for n in range(4):
        loads[n].wait()
    tokens = tok[...]
    pq = jnp.dot(tokens, wq[...], preferred_element_type=F32)
    pkv = jnp.dot(tokens, wkv[...], preferred_element_type=F32)
    pr = jnp.dot(tokens, wr[...], preferred_element_type=F32)
    pr = jnp.concatenate([pr, jnp.zeros_like(pr)], axis=1)
    for i in range(16):
        rows = slice(i * RUN, (i + 1) * RUN)
        part[i // 4, i % 4, :, 0:QL] = pq[rows]
        part[i // 4, i % 4, :, QL : QL + KVL] = pkv[rows]
        part[i // 4, i % 4, :, QL + KVL : WIDE] = pr[rows]

    pl.semaphore_wait(barrier, len(friends))

    def ring_sum(ring, plus, minus, slab, bufs, base, done):
        me, nxt, prv, opp = ring
        L1, L2, L3, R1, R2, R3 = bufs
        send(slab(opp, 0), L1, plus, base)
        send(slab(opp, 1), R1, minus, base + 1)
        send(slab(nxt, 1), L2, plus, base + 2)
        send(slab(prv, 0), R2, minus, base + 3)
        yield
        arrived(L1, base)
        slab(nxt, 0)[...] = slab(nxt, 0)[...] + L1[...]
        send(slab(nxt, 0), L3, plus, base + 4)
        yield
        arrived(R1, base + 1)
        slab(prv, 1)[...] = slab(prv, 1)[...] + R1[...]
        send(slab(prv, 1), R3, minus, base + 5)
        yield
        for buf, k in ((L2, 2), (R2, 3), (L3, 4), (R3, 5)):
            arrived(buf, base + k)
        done(slab(me, 0)[...] + L3[...] + R2[...], slab(me, 1)[...] + L2[...] + R3[...])

    def color(n):
        (a0, aw), (b0, bw) = CUTS[n]
        first = (x, xp, xm, xo), x_plus, x_minus
        second = (y, yp, ym, yo), y_plus, y_minus
        if n == 1:
            first, second = second, first
        mid = mid_y if n else mid_x
        bufs1 = (l1y, l2y, l3y, r1y, r2y, r3y) if n else (l1x, l2x, l3x, r1x, r2x, r3x)
        bufs2 = (k1y, k2y, k3y, j1y, j2y, j3y) if n else (k1x, k2x, k3x, j1x, j2x, j3x)

        def slab1(i, half):
            cols = pl.ds(a0, aw) if half == 0 else pl.ds(b0, bw)
            return part.at[:, i, :, cols] if n else part.at[i, :, :, cols]

        def done1(a, b):
            mid[:, :, 0:aw] = a
            mid[:, :, aw : aw + bw] = b

        yield from ring_sum(*first, slab1, bufs1, fresh(6), done1)
        yield

        def slab2(i, half):
            return mid.at[i, :, pl.ds(0, aw)] if half == 0 else mid.at[i, :, pl.ds(aw, bw)]

        def done2(a, b):
            total[:, a0 : a0 + aw] = a
            total[:, b0 : b0 + bw] = b

        yield from ring_sum(*second, slab2, bufs2, fresh(6), done2)

    def run(tasks):
        tasks = list(tasks)
        while tasks:
            for task in list(tasks):
                try:
                    next(task)
                except StopIteration:
                    tasks.remove(task)

    run([color(0), color(1)])

    def normed(v, gain, width):
        mean_sq = jnp.sum(v * v, axis=1, keepdims=True) / width
        return (v * lax.rsqrt(mean_sq + EPS) * gain).astype(BF16)

    at_run = pos_ref[t * RUN]
    where_at = at_run + lax.broadcasted_iota(jnp.int32, (RUN, 128), 0)
    angle = where_at.astype(F32) * freq_ref[...]
    key = turned(total[:, QL + KVL : WIDE], jnp.cos(angle), jnp.sin(angle))
    lane = lax.broadcasted_iota(jnp.int32, (RUN, 128), 1)
    high = (where_at >> 6).astype(F32)
    low = (where_at & 63).astype(F32)
    key = jnp.where(lane == 64, high, jnp.where(lane == 65, low, key)).astype(BF16)

    def spot(zz):
        hue = zz // 4
        return hue, (1 - hue) * (x * 4 + y) + hue * (y * 4 + x), zz % 4

    hue, place, zrow = spot(z)
    keys[hue, place, c, zrow, :, 0:KVL] = normed(total[:, QL : QL + KVL], gkv_ref[...], KVL)
    keys[hue, place, c, zrow, :, KVL:LINE] = key
    lat_q[t] = normed(total[:, 0:QL], gq_ref[...], QL)

    zbase = fresh(7)
    mine = keys.at[hue, place, c, zrow]
    for d in range(1, 8):
        send(mine, mine, z_peers[d - 1], zbase + d - 1)

    def ring_gather(ring, plus, minus, unit, half, base, got):
        me, nxt, prv, opp = ring
        send(unit(me), unit(me), plus, base)
        send(unit(me), unit(me), minus, base + 1)
        got(me)
        yield
        arrived(unit(prv), base)
        send(half(prv, 0), half(prv, 0), plus, base + 2)
        got(prv)
        yield
        arrived(unit(nxt), base + 1)
        send(half(nxt, 1), half(nxt, 1), minus, base + 3)
        got(nxt)
        yield
        arrived(half(opp, 0), base + 2)
        arrived(half(opp, 1), base + 3)
        got(opp)

    def plane_gather(n, unit, half, tasks, got):
        first = (x, xp, xm, xo), x_plus, x_minus
        second = (y, yp, ym, yo), y_plus, y_minus
        if n == 1:
            first, second = second, first
        other = second[0][0]

        def got1(i):
            def unit2(j):
                return unit(i, j)

            def half2(j, h):
                return half(i, j, h)

            tasks.append(ring_gather(*second, unit2, half2, fresh(4), lambda j: got(i, j)))

        return ring_gather(*first, lambda i: unit(i, other), lambda i, h: half(i, other, h), fresh(4), got1)

    def run_growing(tasks):
        while tasks:
            for task in list(tasks):
                try:
                    next(task)
                except StopIteration:
                    tasks.remove(task)

    tasks = []
    for n in range(2):
        def q_unit(i, j, n=n):
            return lat_q.at[(j * 4 + i) if n else (i * 4 + j), :, pl.ds(768 * n, 768)]

        def q_half(i, j, h, n=n):
            return lat_q.at[(j * 4 + i) if n else (i * 4 + j), :, pl.ds(768 * n + 384 * h, 384)]

        tasks.append(plane_gather(n, q_unit, q_half, tasks, lambda i, j: None))
    run_growing(tasks)

    for d in range(1, 8):
        h2, p2, r2 = spot((z + 8 - d) % 8)
        arrived(keys.at[h2, p2, c, r2], zbase + d - 1)

    tasks = []
    pairs = []
    for n in range(2):
        def k_unit(i, j, n=n):
            return keys.at[n, i * 4 + j, c]

        def k_half(i, j, h, n=n):
            return keys.at[n, i * 4 + j, c, pl.ds(2 * h, 2)]

        def k_got(i, j, n=n):
            k = fresh(1)
            send(keys.at[n, i * 4 + j, c], keys.at[n, i * 4 + j, c], sibling, k)
            pairs.append((keys.at[n, i * 4 + j, 1 - c], k))

        tasks.append(plane_gather(n, k_unit, k_half, tasks, k_got))
    run_growing(tasks)
    for ref, k in pairs:
        arrived(ref, k)

    loads[4].wait()
    loads[5].wait()
    query = jnp.dot(lat_q[...].reshape(16 * RUN, QL), uq[...], preferred_element_type=F32)
    qpos = jnp.concatenate(
        [pos_ref[i * RUN] + lax.broadcasted_iota(jnp.int32, (RUN, 128), 0) for i in range(16)], axis=0
    ).astype(F32)
    qangle = qpos * freq_ref[...]
    qcos, qsin = jnp.cos(qangle), jnp.sin(qangle)
    for h in range(HEAD_DEV):
        qcat[h, :, 0:128] = query[:, 192 * h : 192 * h + 128].astype(BF16)
        tail = query[:, 192 * h + 128 : 192 * h + 192]
        tail = jnp.concatenate([tail, jnp.zeros_like(tail)], axis=1)
        qcat[h, :, 128:256] = turned(tail, qcos, qsin).astype(BF16)
    m_ref[...] = jnp.full_like(m_ref, -1e30)
    l_ref[...] = jnp.zeros_like(l_ref)
    acc_ref[...] = jnp.zeros_like(acc_ref)
    scale = np.float32((1.0 + 0.1 * np.log(40.0)) ** 2 / np.sqrt(192.0))
    qcol = qpos[:, 0:1]
    lane8 = lax.broadcasted_iota(jnp.int32, (8, 128), 1)
    pick = jnp.where(lane8 == 64, 64.0, jnp.where(lane8 == 65, 1.0, 0.0)).astype(BF16)

    def chunk(n, o):
        rows = keys[n, pl.ds(o * 4, 4)].reshape(CHUNK, LINE)
        rope_rows = rows[:, KVL:LINE]
        up = jnp.dot(rows[:, 0:KVL], ukv[...], preferred_element_type=F32).astype(BF16)
        kpos = lax.dot_general(pick, rope_rows, (((1,), (1,)), ((), ())), preferred_element_type=F32)[0:1]
        seen = kpos <= qcol
        for h in range(HEAD_DEV):
            kcat = jnp.concatenate([up[:, 256 * h : 256 * h + 128], rope_rows], axis=1)
            sc = lax.dot_general(qcat[h], kcat, (((1,), (1,)), ((), ())), preferred_element_type=F32)
            sc = jnp.where(seen, sc * scale, -1e30)
            old = m_ref[h]
            new = jnp.maximum(old, jnp.max(sc, axis=1, keepdims=True))
            fade = jnp.exp(old - new)
            w = jnp.exp(sc - new)
            m_ref[h] = new
            l_ref[h] = l_ref[h] * fade + jnp.sum(w, axis=1, keepdims=True)
            acc_ref[h] = acc_ref[h] * fade + jnp.dot(
                w.astype(BF16), up[:, 256 * h + 128 : 256 * h + 256], preferred_element_type=F32
            )

    def step(i, _):
        chunk(i // 4, i % 4)
        return 0

    lax.fori_loop(0, 8, step, 0)
    for h in range(HEAD_DEV):
        out_ref[:, VDIM * h : VDIM * (h + 1)] = (acc_ref[h] / l_ref[h]).astype(BF16)

    for copy in sent:
        copy.wait_send()
    assert count[0] <= SEMS, count[0]


SEMS = 160
FREQ = np.zeros((1, 128), np.float32)
FREQ[0, :64] = np.tile(
    np.float32(10000.0) ** (-(np.arange(32, dtype=np.float32) * np.float32(2.0) / np.float32(64))), 2
)


def body(tokens, positions, w_down_q, w_down_kv, w_rope_key, gain_query, gain_kv, w_up_q, w_up_kv):
    vmem = pl.BlockSpec(memory_space=pltpu.VMEM)
    smem = pl.BlockSpec(memory_space=pltpu.SMEM)
    any_ = pl.BlockSpec(memory_space=pl.ANY)

    def sums(lead, n):
        (_, aw), (_, bw) = CUTS[n]
        return [pltpu.VMEM(lead + (w,), F32) for w in (aw, bw, aw, bw, aw, bw)]

    scratch = (
        [pltpu.VMEM(a.shape, a.dtype) for a in (tokens, w_down_q, w_down_kv, w_rope_key, w_up_q, w_up_kv)]
        + [pltpu.VMEM((4, 4, RUN, WIDE), F32)]
        + sums((4, RUN), 0)
        + sums((4, RUN), 1)
        + [pltpu.VMEM((4, RUN, 1152), F32), pltpu.VMEM((4, RUN, 1024), F32)]
        + sums((RUN,), 0)
        + sums((RUN,), 1)
        + [
            pltpu.VMEM((RUN, WIDE), F32),
            pltpu.VMEM((16, RUN, QL), BF16),
            pltpu.VMEM((2, 16, 2, 4, RUN, LINE), BF16),
            pltpu.VMEM((HEAD_DEV, 256, 256), BF16),
            pltpu.VMEM((HEAD_DEV, 256, 1), F32),
            pltpu.VMEM((HEAD_DEV, 256, 1), F32),
            pltpu.VMEM((HEAD_DEV, 256, VDIM), F32),
            pltpu.SemaphoreType.DMA((6,)),
            pltpu.SemaphoreType.DMA((SEMS,)),
            pltpu.SemaphoreType.DMA((SEMS,)),
        ]
    )
    return pl.pallas_call(
        kernel,
        out_shape=jax.ShapeDtypeStruct((256, HEAD_DEV * VDIM), BF16),
        in_specs=[smem, vmem, vmem, vmem] + [any_] * 6,
        out_specs=vmem,
        scratch_shapes=scratch,
        compiler_params=pltpu.CompilerParams(
            collective_id=0, has_side_effects=True, vmem_limit_bytes=56 * 1024 * 1024
        ),
    )(
        positions, jnp.asarray(FREQ), gain_query.reshape(1, QL), gain_kv.reshape(1, KVL),
        tokens, w_down_q, w_down_kv, w_rope_key, w_up_q, w_up_kv,
    )


def solution(mesh):
    in_specs = (
        P("seq", "tensor"),
        P("seq"),
        P("tensor", None),
        P("tensor", None),
        P("tensor", None),
        P(),
        P(),
        P(None, "tensor"),
        P(None, "tensor"),
    )
    out_specs = P("seq", "tensor")
    return jax.shard_map(body, mesh=mesh, in_specs=in_specs, out_specs=out_specs, check_vma=False)
```

```python
import functools

import numpy as np
import jax
import jax.numpy as jnp
from jax import lax
from jax.experimental import pallas as pl
from jax.experimental.pallas import tpu as pltpu
from jax.sharding import PartitionSpec as P

NOPE = 128
ROPE = 64
VDIM = 128
HEAD_DEV = 4
QL = 1536
KVL = 512
LINE = KVL + 128
RUN = 16
GROUP = 512
MESH = pl.DeviceIdType.MESH
EPS = 1e-06
F32 = jnp.float32
BF16 = jnp.bfloat16

CUTS_Q = (((0, 384), (384, 384)), ((768, 384), (1152, 384)))
CUTS_K = (((0, 128), (128, 128)), ((256, 256), (512, 128)))


def turned(v, cosine, sine):
    lane = lax.broadcasted_iota(jnp.int32, v.shape, 1)
    swapped = jnp.where(lane < 32, -pltpu.roll(v, 96, 1), pltpu.roll(v, 32, 1))
    return jnp.where(lane < 64, v * cosine + swapped * sine, 0.0)


def kernel(
    pos_ref, freq_ref, gq_ref, gkv_ref, tok_hbm, wq_hbm, wkv_hbm, wr_hbm, uq_hbm, ukv_hbm,
    out_ref,
    tok, wq, wkv, wr, uq, ukv,
    part_q, part_k, bufs_q, bufs_k, mids_q, mids_k, small_q, small_k,
    total_q, total_k, lat_q, keys, up_ref, rope_ref, qcat, m_ref, l_ref, acc_ref,
    load_sem, send_sem, recv_sem,
):
    s = lax.axis_index("seq")
    t = lax.axis_index("tensor")
    x, y = t // 4, t % 4
    z, c = s // 2, s % 2

    loads = []
    for n, (a, b) in enumerate(
        ((tok_hbm, tok), (wkv_hbm, wkv), (wr_hbm, wr), (wq_hbm, wq), (uq_hbm, uq), (ukv_hbm, ukv))
    ):
        loads.append(pltpu.make_async_copy(a, b, load_sem.at[n]))
        loads[-1].start()

    def at(xx, yy):
        return (s, xx * 4 + yy)

    ring_x = (x, (x + 1) % 4, (x + 3) % 4, (x + 2) % 4)
    ring_y = (y, (y + 1) % 4, (y + 3) % 4, (y + 2) % 4)
    along_x = ring_x, at(ring_x[1], y), at(ring_x[2], y)
    along_y = ring_y, at(x, ring_y[1]), at(x, ring_y[2])
    sibling = (s + 1 - 2 * c, t)
    z_peers = [(((z + d) % 8) * 2 + c, t) for d in range(1, 8)]

    barrier = pltpu.get_barrier_semaphore()
    friends = [*along_x[1:], *along_y[1:], sibling] + z_peers
    for who in friends:
        pl.semaphore_signal(barrier, inc=1, device_id=who, device_id_type=MESH)

    sent = []
    count = [0]

    def fresh(n):
        count[0] += n
        return count[0] - n

    def send(src, dst, who, k):
        copy = pltpu.make_async_remote_copy(
            src_ref=src, dst_ref=dst, send_sem=send_sem.at[k], recv_sem=recv_sem.at[k],
            device_id=who, device_id_type=MESH,
        )
        copy.start()
        sent.append(copy)

    def arrived(dst, k):
        pltpu.make_async_remote_copy(
            src_ref=dst, dst_ref=dst, send_sem=send_sem.at[k], recv_sem=recv_sem.at[k],
            device_id=sibling, device_id_type=MESH,
        ).wait_recv()

    def ring_sum(along, slab, bufs, done, split):
        (me, nxt, prv, opp), plus, minus = along
        L1, L2, L3, R1, R2, R3 = bufs
        base = fresh(6)
        send(slab(opp, 0), L1, plus, base)
        send(slab(opp, 1), R1, minus, base + 1)
        if split:
            yield
        send(slab(nxt, 1), L2, plus, base + 2)
        send(slab(prv, 0), R2, minus, base + 3)
        yield
        arrived(L1, base)
        slab(nxt, 0)[...] = slab(nxt, 0)[...] + L1[...]
        send(slab(nxt, 0), L3, plus, base + 4)
        arrived(R1, base + 1)
        slab(prv, 1)[...] = slab(prv, 1)[...] + R1[...]
        send(slab(prv, 1), R3, minus, base + 5)
        yield
        for buf, k in ((L2, 2), (R2, 3), (L3, 4), (R3, 5)):
            arrived(buf, base + k)
        done(slab(me, 0)[...] + L3[...] + R2[...], slab(me, 1)[...] + L2[...] + R3[...])

    def summed(n, cuts, part, bufs, mid, small, total, split):
        (a0, aw), (b0, bw) = cuts[n]
        first, second = (along_y, along_x) if n else (along_x, along_y)

        def slab1(i, half):
            cols = pl.ds(b0, bw) if half else pl.ds(a0, aw)
            return part.at[:, i, :, cols] if n else part.at[i, :, :, cols]

        def slab2(i, half):
            return mid.at[i, :, pl.ds(aw, bw) if half else pl.ds(0, aw)]

        def done1(a, b):
            mid[:, :, 0:aw] = a
            mid[:, :, aw : aw + bw] = b

        def done2(a, b):
            total[:, a0 : a0 + aw] = a
            total[:, b0 : b0 + bw] = b

        yield from ring_sum(first, slab1, bufs, done1, split)
        yield from ring_sum(second, slab2, small, done2, False)

    sum_k = [summed(n, CUTS_K, part_k, bufs_k[n], mids_k[n], small_k[n], total_k, False) for n in range(2)]
    sum_q = [summed(n, CUTS_Q, part_q, bufs_q[n], mids_q[n], small_q[n], total_q, True) for n in range(2)]

    def go(tasks):
        for task in tasks:
            next(task, None)

    loads[0].wait()
    loads[1].wait()
    loads[2].wait()
    tokens = tok[...].T
    pk = jnp.dot(tokens, wkv[...], preferred_element_type=F32)
    pr = lax.dot_general(tokens, wr[...], (((1,), (1,)), ((), ())), preferred_element_type=F32)
    pr = jnp.concatenate([pr, jnp.zeros_like(pr)], axis=1)
    for i in range(16):
        rows = slice(i * RUN, (i + 1) * RUN)
        part_k[i // 4, i % 4, :, 0:KVL] = pk[rows]
        part_k[i // 4, i % 4, :, KVL:LINE] = pr[rows]
    pl.semaphore_wait(barrier, len(friends))
    go(sum_k)

    loads[3].wait()
    pq = jnp.dot(tokens, wq[...], preferred_element_type=F32)
    for i in range(16):
        part_q[i // 4, i % 4] = pq[i * RUN : (i + 1) * RUN]
    go(sum_q)
    go(sum_k)
    go(sum_q)
    go(sum_k)
    go(sum_q)
    go(sum_k)
    go(sum_q)

    def normed(v, gain, width):
        mean_sq = jnp.sum(v * v, axis=1, keepdims=True) / width
        return (v * lax.rsqrt(mean_sq + EPS) * gain).astype(BF16)

    at_run = pos_ref[t * RUN]
    where_at = at_run + lax.broadcasted_iota(jnp.int32, (RUN, 128), 0)
    angle = where_at.astype(F32) * freq_ref[...]
    cosine, sine = jnp.cos(angle), jnp.sin(angle)
    lane = lax.broadcasted_iota(jnp.int32, (RUN, 128), 1)
    high = (where_at >> 6).astype(F32)
    low = (where_at & 63).astype(F32)

    go(sum_k)
    key = turned(total_k[:, KVL:LINE], cosine, sine)
    key = jnp.where(lane == 64, high, jnp.where(lane == 65, low, key)).astype(BF16)

    def spot(zz):
        hue = zz // 4
        return hue, (1 - hue) * (x * 4 + y) + hue * (y * 4 + x), zz % 4

    hue, place, zrow = spot(z)
    keys[hue, place, c, zrow, :, 0:KVL] = normed(total_k[:, 0:KVL], gkv_ref[...], KVL)
    keys[hue, place, c, zrow, :, KVL:LINE] = key

    zbase = fresh(7)
    mine = keys.at[hue, place, c, zrow]
    for d in range(1, 8):
        send(mine, mine, z_peers[d - 1], zbase + d - 1)

    class Gather:
        def __init__(self, n, unit, half, got):
            self.first, self.second = (along_y, along_x) if n else (along_x, along_y)
            self.unit, self.half, self.got = unit, half, got
            self.base1 = fresh(4)
            self.base2 = [fresh(4) for _ in range(4)]

        def name(self, i, j):
            return self.first[0][i], self.second[0][j]

        def start2(self, i):
            u = self.unit(*self.name(i, 0))
            send(u, u, self.second[1], self.base2[i])
            send(u, u, self.second[2], self.base2[i] + 1)
            self.got(*self.name(i, 0))

        def start(self):
            u = self.unit(*self.name(0, 0))
            send(u, u, self.first[1], self.base1)
            send(u, u, self.first[2], self.base1 + 1)
            self.start2(0)

        def take(self, where, pick, base, along):
            if pick == 3:
                arrived(self.half(*where, 0), base + 2)
                arrived(self.half(*where, 1), base + 3)
            elif pick == 2:
                arrived(self.unit(*where), base)
                h = self.half(*where, 0)
                send(h, h, along[1], base + 2)
            else:
                arrived(self.unit(*where), base + 1)
                h = self.half(*where, 1)
                send(h, h, along[2], base + 3)

        def arrive1(self, i):
            self.take(self.name(i, 0), i, self.base1, self.first)
            self.start2(i)

        def arrive2(self, i, j):
            self.take(self.name(i, j), j, self.base2[i], self.second)
            self.got(*self.name(i, j))

    pairs = {}

    def gather_q(n):
        def unit(i, j):
            return lat_q.at[(j * 4 + i) if n else (i * 4 + j), :, pl.ds(768 * n, 768)]

        def half(i, j, h):
            return lat_q.at[(j * 4 + i) if n else (i * 4 + j), :, pl.ds(768 * n + 384 * h, 384)]

        return Gather(n, unit, half, lambda i, j: None)

    def gather_k(n):
        def unit(i, j):
            return keys.at[n, i * 4 + j, c]

        def half(i, j, h):
            return keys.at[n, i * 4 + j, c, pl.ds(2 * h, 2)]

        def got(i, j):
            k = fresh(1)
            send(unit(i, j), unit(i, j), sibling, k)
            pairs.setdefault(n, []).append((keys.at[n, i * 4 + j, 1 - c], k))

        return Gather(n, unit, half, got)

    go(sum_q)
    go(sum_q)
    gain_q = jnp.concatenate([gq_ref[i : i + 1, :] for i in range(QL // 128)], axis=1)
    lat_q[t] = normed(total_q[...], gain_q, QL)

    gq = [gather_q(n) for n in range(2)]
    gk = [gather_k(n) for n in range(2)]
    for g in gq:
        g.start()
    for d in range(1, 8):
        h2, p2, r2 = spot((z + 8 - d) % 8)
        arrived(keys.at[h2, p2, c, r2], zbase + d - 1)
    for g in gk:
        g.start()

    scale = np.float32((1.0 + 0.1 * np.log(40.0)) ** 2 / np.sqrt(192.0))
    lane8 = lax.broadcasted_iota(jnp.int32, (8, 128), 1)
    pick = jnp.where(lane8 == 64, 64.0, jnp.where(lane8 == 65, 1.0, 0.0)).astype(BF16)
    m_ref[...] = jnp.full_like(m_ref, -1e30)
    l_ref[...] = jnp.zeros_like(l_ref)
    acc_ref[...] = jnp.zeros_like(acc_ref)
    qpos = jnp.concatenate(
        [pos_ref[i * RUN] + lax.broadcasted_iota(jnp.int32, (RUN, 128), 0) for i in range(16)], axis=0
    ).astype(F32)
    qcol = qpos[:, 0:1]

    def queries():
        query = jnp.dot(lat_q[...].reshape(16 * RUN, QL), uq[...], preferred_element_type=F32)
        qangle = qpos * freq_ref[...]
        qcos, qsin = jnp.cos(qangle), jnp.sin(qangle)
        for h in range(HEAD_DEV):
            qcat[h, :, 0:128] = query[:, 192 * h : 192 * h + 128].astype(BF16)
            tail = query[:, 192 * h + 128 : 192 * h + 192]
            tail = jnp.concatenate([tail, jnp.zeros_like(tail)], axis=1)
            qcat[h, :, 128:256] = turned(tail, qcos, qsin).astype(BF16)

    groups = (
        ((0, 0), (2, 0)), ((1, 0), (0, 2)), ((0, 1), (3, 0)), ((2, 2), (2, 1)),
        ((1, 2), (1, 1)), ((0, 3), (3, 2)), ((3, 1), (2, 3)), ((1, 3), (3, 3)),
    )
    def expand(g):
        rows = []
        for n in range(2):
            for i, j in groups[g]:
                p, q = gk[n].name(i, j)
                ref, k = pairs[n][sequence.index((i, j))]
                arrived(ref, k)
                rows.append(keys[n, p * 4 + q].reshape(128, LINE))
        rows = jnp.concatenate(rows, axis=0)
        rope_ref[g] = rows[:, KVL:LINE]
        up_ref[g] = jnp.dot(rows[:, 0:KVL], ukv[...], preferred_element_type=F32).astype(BF16)

    def attend(g):
        rope_rows = rope_ref[g]
        kpos = lax.dot_general(pick, rope_rows, (((1,), (1,)), ((), ())), preferred_element_type=F32)[0:1]
        seen = kpos <= qcol
        for h in range(HEAD_DEV):
            kcat = jnp.concatenate([up_ref[g, :, 256 * h : 256 * h + 128], rope_rows], axis=1)
            sc = lax.dot_general(qcat[h], kcat, (((1,), (1,)), ((), ())), preferred_element_type=F32)
            sc = jnp.where(seen, sc * scale, -1e30)
            old = m_ref[h]
            new = jnp.maximum(old, jnp.max(sc, axis=1, keepdims=True))
            fade = jnp.exp(old - new)
            w = jnp.exp(sc - new)
            m_ref[h] = new
            l_ref[h] = l_ref[h] * fade + jnp.sum(w, axis=1, keepdims=True)
            acc_ref[h] = acc_ref[h] * fade + jnp.dot(
                w.astype(BF16), up_ref[g, :, 256 * h + 128 : 256 * h + 256], preferred_element_type=F32
            )

    sequence = [(0, 0)]

    def k_step(*steps):
        for step in steps:
            for g in gk:
                if isinstance(step, int):
                    g.arrive1(step)
                else:
                    g.arrive2(*step)
            sequence.append((step, 0) if isinstance(step, int) else step)

    def q_step(*steps):
        for step in steps:
            for g in gq:
                if isinstance(step, int):
                    g.arrive1(step)
                else:
                    g.arrive2(*step)

    q_step(2, 1)
    q_step((0, 2), (0, 1))
    k_step(2, 1)
    q_step(3)
    k_step((0, 2), (0, 1), 3)
    q_step((2, 2), (2, 1), (1, 2), (1, 1), (0, 3))
    loads[5].wait()
    expand(0)
    k_step((2, 2), (2, 1), (1, 2), (1, 1))
    q_step((3, 2), (3, 1), (2, 3), (1, 3))
    expand(1)
    k_step((0, 3), (3, 2), (3, 1))
    q_step((3, 3))
    loads[4].wait()
    queries()
    attend(0)
    expand(2)
    attend(1)
    k_step((2, 3), (1, 3), (3, 3))
    attend(2)
    for g in range(3, 8):
        expand(g)
        attend(g)
    for h in range(HEAD_DEV):
        out_ref[:, VDIM * h : VDIM * (h + 1)] = (acc_ref[h] / l_ref[h]).astype(BF16)

    for copy in sent:
        copy.wait_send()
    assert count[0] <= SEMS, count[0]


SEMS = 176
FREQ = np.zeros((1, 128), np.float32)
FREQ[0, :64] = np.tile(
    np.float32(10000.0) ** (-(np.arange(32, dtype=np.float32) * np.float32(2.0) / np.float32(64))), 2
)


def body(tokens, positions, w_down_q, w_down_kv, w_rope_key, gain_query, gain_kv, w_up_q, w_up_kv):
    vmem = pl.BlockSpec(memory_space=pltpu.VMEM)
    smem = pl.BlockSpec(memory_space=pltpu.SMEM)
    any_ = pl.BlockSpec(memory_space=pl.ANY)

    def sums(lead, cuts):
        out = []
        for (_, aw), (_, bw) in cuts:
            out.append([pltpu.VMEM(lead + (w,), F32) for w in (aw, bw, aw, bw, aw, bw)])
        return out

    def mids(cuts):
        return [pltpu.VMEM((4, RUN, a[1] + b[1]), F32) for a, b in cuts]

    tokens, w_rope_key = tokens.T, w_rope_key.T
    scratch = (
        [pltpu.VMEM(a.shape, a.dtype) for a in (tokens, w_down_q, w_down_kv, w_rope_key, w_up_q, w_up_kv)]
        + [pltpu.VMEM((4, 4, RUN, QL), F32), pltpu.VMEM((4, 4, RUN, LINE), F32)]
        + [sums((4, RUN), CUTS_Q), sums((4, RUN), CUTS_K), mids(CUTS_Q), mids(CUTS_K)]
        + [sums((RUN,), CUTS_Q), sums((RUN,), CUTS_K)]
        + [
            pltpu.VMEM((RUN, QL), F32),
            pltpu.VMEM((RUN, LINE), F32),
            pltpu.VMEM((16, RUN, QL), BF16),
            pltpu.VMEM((2, 16, 2, 4, RUN, LINE), BF16),
            pltpu.VMEM((8, GROUP, 1024), BF16),
            pltpu.VMEM((8, GROUP, 128), BF16),
            pltpu.VMEM((HEAD_DEV, 256, 256), BF16),
            pltpu.VMEM((HEAD_DEV, 256, 1), F32),
            pltpu.VMEM((HEAD_DEV, 256, 1), F32),
            pltpu.VMEM((HEAD_DEV, 256, VDIM), F32),
            pltpu.SemaphoreType.DMA((6,)),
            pltpu.SemaphoreType.DMA((SEMS,)),
            pltpu.SemaphoreType.DMA((SEMS,)),
        ]
    )
    return pl.pallas_call(
        kernel,
        out_shape=jax.ShapeDtypeStruct((256, HEAD_DEV * VDIM), BF16),
        in_specs=[smem, vmem, vmem, vmem] + [any_] * 6,
        out_specs=vmem,
        scratch_shapes=scratch,
        compiler_params=pltpu.CompilerParams(
            collective_id=0, has_side_effects=True, vmem_limit_bytes=56 * 1024 * 1024
        ),
    )(
        positions, jnp.asarray(FREQ), gain_query.reshape(QL // 128, 128), gain_kv.reshape(1, KVL),
        tokens, w_down_q, w_down_kv, w_rope_key, w_up_q, w_up_kv,
    )


def solution(mesh):
    in_specs = (
        P("seq", "tensor"),
        P("seq"),
        P("tensor", None),
        P("tensor", None),
        P("tensor", None),
        P(),
        P(),
        P(None, "tensor"),
        P(None, "tensor"),
    )
    out_specs = P("seq", "tensor")
    return jax.shard_map(body, mesh=mesh, in_specs=in_specs, out_specs=out_specs, check_vma=False)
```

```python
import functools

import numpy as np
import jax
import jax.numpy as jnp
from jax import lax
from jax.experimental import pallas as pl
from jax.experimental.pallas import tpu as pltpu
from jax.sharding import PartitionSpec as P

NOPE = 128
ROPE = 64
VDIM = 128
HEAD_DEV = 4
QL = 1536
KVL = 512
LINE = KVL + 128
RUN = 16
GROUP = 512
MESH = pl.DeviceIdType.MESH
EPS = 1e-06
F32 = jnp.float32
BF16 = jnp.bfloat16

CUTS_Q = (((0, 384), (384, 384)), ((768, 384), (1152, 384)))
CUTS_K = (((0, 128), (128, 128)), ((256, 256), (512, 128)))


def turned(v, cosine, sine):
    lane = lax.broadcasted_iota(jnp.int32, v.shape, 1)
    swapped = jnp.where(lane < 32, -pltpu.roll(v, 96, 1), pltpu.roll(v, 32, 1))
    return jnp.where(lane < 64, v * cosine + swapped * sine, 0.0)


def kernel(
    pos_ref, freq_hbm, gq_hbm, gkv_hbm, tok_hbm, wq_hbm, wkv_hbm, wr_hbm, uq_hbm, ukv_hbm,
    out_ref,
    tok, wq, wkv, wr, uq, ukv, freq_ref, gq_ref, gkv_ref,
    part_q, part_k, bufs_q, bufs_k, mids_q, mids_k, small_q, small_k,
    total_q, total_k, lat_q, keys, up_ref, rope_ref, qcat, m_ref, l_ref, acc_ref,
    load_sem, send_sem, recv_sem, near_sem,
):
    s = lax.axis_index("seq")
    t = lax.axis_index("tensor")
    x, y = t // 4, t % 4
    z, c = s // 2, s % 2

    loads = []
    for n, (a, b) in enumerate(
        (
            (tok_hbm, tok), (wkv_hbm, wkv), (wr_hbm, wr), (wq_hbm, wq), (uq_hbm, uq), (ukv_hbm, ukv),
            (freq_hbm, freq_ref), (gq_hbm, gq_ref), (gkv_hbm, gkv_ref),
        )
    ):
        loads.append(pltpu.make_async_copy(a, b, load_sem.at[n]))
        loads[-1].start()

    def at(xx, yy):
        return (s, xx * 4 + yy)

    ring_x = (x, (x + 1) % 4, (x + 3) % 4, (x + 2) % 4)
    ring_y = (y, (y + 1) % 4, (y + 3) % 4, (y + 2) % 4)
    along_x = ring_x, at(ring_x[1], y), at(ring_x[2], y)
    along_y = ring_y, at(x, ring_y[1]), at(x, ring_y[2])
    sibling = (s + 1 - 2 * c, t)
    z_peers = [(((z + d) % 8) * 2 + c, t) for d in range(1, 8)]

    barrier = pltpu.get_barrier_semaphore()
    friends = [*along_x[1:], *along_y[1:], sibling, z_peers[0], z_peers[6]]
    for who in friends:
        pl.semaphore_signal(barrier, inc=1, device_id=who, device_id_type=MESH)

    sent = []
    count = [0]

    def fresh(n):
        count[0] += n
        return count[0] - n

    def send(src, dst, who, k):
        copy = pltpu.make_async_remote_copy(
            src_ref=src, dst_ref=dst, send_sem=send_sem.at[k], recv_sem=recv_sem.at[k],
            device_id=who, device_id_type=MESH,
        )
        copy.start()
        sent.append(copy)

    def arrived(dst, k):
        pltpu.make_async_remote_copy(
            src_ref=dst, dst_ref=dst, send_sem=send_sem.at[k], recv_sem=recv_sem.at[k],
            device_id=sibling, device_id_type=MESH,
        ).wait_recv()

    def ring_sum(along, slab, bufs, done, split):
        (me, nxt, prv, opp), plus, minus = along
        L1, L2, L3, R1, R2, R3 = bufs
        base = fresh(6)
        send(slab(opp, 0), L1, plus, base)
        send(slab(opp, 1), R1, minus, base + 1)
        if split:
            yield
        send(slab(nxt, 1), L2, plus, base + 2)
        send(slab(prv, 0), R2, minus, base + 3)
        yield
        arrived(L1, base)
        slab(nxt, 0)[...] = slab(nxt, 0)[...] + L1[...]
        send(slab(nxt, 0), L3, plus, base + 4)
        arrived(R1, base + 1)
        slab(prv, 1)[...] = slab(prv, 1)[...] + R1[...]
        send(slab(prv, 1), R3, minus, base + 5)
        yield
        for buf, k in ((L2, 2), (R2, 3), (L3, 4), (R3, 5)):
            arrived(buf, base + k)
        done(slab(me, 0)[...] + L3[...] + R2[...], slab(me, 1)[...] + L2[...] + R3[...])

    def summed(n, cuts, part, bufs, mid, small, total, split):
        (a0, aw), (b0, bw) = cuts[n]
        first, second = (along_y, along_x) if n else (along_x, along_y)

        def slab1(i, half):
            cols = pl.ds(b0, bw) if half else pl.ds(a0, aw)
            return part.at[:, i, :, cols] if n else part.at[i, :, :, cols]

        def slab2(i, half):
            return mid.at[i, :, pl.ds(aw, bw) if half else pl.ds(0, aw)]

        def done1(a, b):
            mid[:, :, 0:aw] = a
            mid[:, :, aw : aw + bw] = b

        def done2(a, b):
            total[:, a0 : a0 + aw] = a
            total[:, b0 : b0 + bw] = b

        yield from ring_sum(first, slab1, bufs, done1, split)
        yield from ring_sum(second, slab2, small, done2, False)

    sum_k = [summed(n, CUTS_K, part_k, bufs_k[n], mids_k[n], small_k[n], total_k, False) for n in range(2)]
    sum_q = [summed(n, CUTS_Q, part_q, bufs_q[n], mids_q[n], small_q[n], total_q, True) for n in range(2)]

    def go(tasks):
        for task in tasks:
            next(task, None)

    loads[0].wait()
    loads[1].wait()
    loads[2].wait()
    tokens = tok[...].T
    pk = jnp.dot(tokens, wkv[...], preferred_element_type=F32)
    pr = lax.dot_general(tokens, wr[...], (((1,), (1,)), ((), ())), preferred_element_type=F32)
    pr = jnp.concatenate([pr, jnp.zeros_like(pr)], axis=1)
    for i in range(16):
        rows = slice(i * RUN, (i + 1) * RUN)
        part_k[i // 4, i % 4, :, 0:KVL] = pk[rows]
        part_k[i // 4, i % 4, :, KVL:LINE] = pr[rows]
    pl.semaphore_wait(barrier, len(friends))

    def tell(hop):
        pl.semaphore_signal(near_sem.at[hop, 0], inc=1, device_id=z_peers[0], device_id_type=MESH)
        pl.semaphore_signal(near_sem.at[hop, 1], inc=1, device_id=z_peers[6], device_id_type=MESH)

    def told(hop):
        pl.semaphore_wait(near_sem.at[hop, 0], 1)
        pl.semaphore_wait(near_sem.at[hop, 1], 1)

    go(sum_k)
    tell(0)

    loads[3].wait()
    pq = jnp.dot(tokens, wq[...], preferred_element_type=F32)
    for i in range(16):
        part_q[i // 4, i % 4] = pq[i * RUN : (i + 1) * RUN]
    go(sum_q)
    go(sum_k)
    go(sum_q)
    told(0)
    tell(1)
    go(sum_k)
    told(1)
    tell(2)
    go(sum_q)
    go(sum_k)
    go(sum_q)

    def normed(v, gain, width):
        mean_sq = jnp.sum(v * v, axis=1, keepdims=True) / width
        return (v * lax.rsqrt(mean_sq + EPS) * gain).astype(BF16)

    told(2)
    for n in (6, 7, 8):
        loads[n].wait()
    at_run = pos_ref[t * RUN]
    where_at = at_run + lax.broadcasted_iota(jnp.int32, (RUN, 128), 0)
    angle = where_at.astype(F32) * freq_ref[...]
    cosine, sine = jnp.cos(angle), jnp.sin(angle)
    lane = lax.broadcasted_iota(jnp.int32, (RUN, 128), 1)
    high = (where_at >> 6).astype(F32)
    low = (where_at & 63).astype(F32)

    go(sum_k)
    key = turned(total_k[:, KVL:LINE], cosine, sine)
    key = jnp.where(lane == 64, high, jnp.where(lane == 65, low, key)).astype(BF16)

    def spot(zz):
        hue = zz // 4
        return hue, (1 - hue) * (x * 4 + y) + hue * (y * 4 + x), zz % 4

    hue, place, zrow = spot(z)
    keys[hue, place, c, zrow, :, 0:KVL] = normed(total_k[:, 0:KVL], gkv_ref[...], KVL)
    keys[hue, place, c, zrow, :, KVL:LINE] = key

    zbase = fresh(7)
    mine = keys.at[hue, place, c, zrow]
    for d in range(1, 8):
        send(mine, mine, z_peers[d - 1], zbase + d - 1)

    class Gather:
        def __init__(self, n, unit, half, got):
            self.first, self.second = (along_y, along_x) if n else (along_x, along_y)
            self.unit, self.half, self.got = unit, half, got
            self.base1 = fresh(4)
            self.base2 = [fresh(4) for _ in range(4)]

        def name(self, i, j):
            return self.first[0][i], self.second[0][j]

        def start2(self, i):
            u = self.unit(*self.name(i, 0))
            send(u, u, self.second[1], self.base2[i])
            send(u, u, self.second[2], self.base2[i] + 1)
            self.got(*self.name(i, 0))

        def start(self):
            u = self.unit(*self.name(0, 0))
            send(u, u, self.first[1], self.base1)
            send(u, u, self.first[2], self.base1 + 1)
            self.start2(0)

        def take(self, where, pick, base, along):
            if pick == 3:
                arrived(self.half(*where, 0), base + 2)
                arrived(self.half(*where, 1), base + 3)
            elif pick == 2:
                arrived(self.unit(*where), base)
                h = self.half(*where, 0)
                send(h, h, along[1], base + 2)
            else:
                arrived(self.unit(*where), base + 1)
                h = self.half(*where, 1)
                send(h, h, along[2], base + 3)

        def arrive1(self, i):
            self.take(self.name(i, 0), i, self.base1, self.first)
            self.start2(i)

        def arrive2(self, i, j):
            self.take(self.name(i, j), j, self.base2[i], self.second)
            self.got(*self.name(i, j))

    pairs = {}

    def gather_q(n):
        def unit(i, j):
            return lat_q.at[(j * 4 + i) if n else (i * 4 + j), :, pl.ds(768 * n, 768)]

        def half(i, j, h):
            return lat_q.at[(j * 4 + i) if n else (i * 4 + j), :, pl.ds(768 * n + 384 * h, 384)]

        return Gather(n, unit, half, lambda i, j: None)

    def gather_k(n):
        def unit(i, j):
            return keys.at[n, i * 4 + j, c]

        def half(i, j, h):
            return keys.at[n, i * 4 + j, c, pl.ds(2 * h, 2)]

        def got(i, j):
            k = fresh(1)
            send(unit(i, j), unit(i, j), sibling, k)
            pairs.setdefault(n, []).append((keys.at[n, i * 4 + j, 1 - c], k))

        return Gather(n, unit, half, got)

    go(sum_q)
    go(sum_q)
    gain_q = jnp.concatenate([gq_ref[i : i + 1, :] for i in range(QL // 128)], axis=1)
    lat_q[t] = normed(total_q[...], gain_q, QL)

    gq = [gather_q(n) for n in range(2)]
    gk = [gather_k(n) for n in range(2)]
    for g in gq:
        g.start()
    for d in range(1, 8):
        h2, p2, r2 = spot((z + 8 - d) % 8)
        arrived(keys.at[h2, p2, c, r2], zbase + d - 1)
    for g in gk:
        g.start()

    scale = np.float32((1.0 + 0.1 * np.log(40.0)) ** 2 / np.sqrt(192.0) / np.log(2.0))
    lane8 = lax.broadcasted_iota(jnp.int32, (8, 128), 1)
    pick = jnp.where(lane8 == 64, 64.0, jnp.where(lane8 == 65, 1.0, 0.0)).astype(BF16)
    qpos = jnp.concatenate(
        [pos_ref[i * RUN] + lax.broadcasted_iota(jnp.int32, (RUN, 128), 0) for i in range(16)], axis=0
    ).astype(F32)
    qcol = qpos[:, 0:1]

    def queries():
        query = jnp.dot(lat_q[...].reshape(16 * RUN, QL), uq[...], preferred_element_type=F32)
        qangle = qpos * freq_ref[...]
        qcos, qsin = jnp.cos(qangle), jnp.sin(qangle)
        for h in range(HEAD_DEV):
            qcat[h, :, 0:128] = query[:, 192 * h : 192 * h + 128].astype(BF16)
            tail = query[:, 192 * h + 128 : 192 * h + 192]
            tail = jnp.concatenate([tail, jnp.zeros_like(tail)], axis=1)
            qcat[h, :, 128:256] = turned(tail, qcos, qsin).astype(BF16)

    groups = (
        ((0, 0), (2, 0)), ((1, 0), (0, 2)), ((0, 1), (3, 0)), ((2, 2), (2, 1)),
        ((1, 2), (1, 1)), ((0, 3), (3, 2)), ((3, 1), (2, 3)), ((1, 3), (3, 3)),
    )
    def expand(g):
        rows = []
        for n in range(2):
            for i, j in groups[g]:
                p, q = gk[n].name(i, j)
                ref, k = pairs[n][sequence.index((i, j))]
                arrived(ref, k)
                rows.append(keys[n, p * 4 + q].reshape(128, LINE))
        rows = jnp.concatenate(rows, axis=0)
        spot_g = pl.ds(g * GROUP, GROUP)
        rope_ref[spot_g] = rows[:, KVL:LINE]
        up_ref[spot_g] = jnp.dot(rows[:, 0:KVL], ukv[...], preferred_element_type=F32).astype(BF16)

    def attend(g, many):
        rows = pl.ds(g * GROUP, many * GROUP)
        rope_rows = rope_ref[rows]
        kpos = lax.dot_general(pick, rope_rows, (((1,), (1,)), ((), ())), preferred_element_type=F32)[0:1]
        seen = kpos <= qcol
        for h in range(HEAD_DEV):
            kcat = jnp.concatenate([up_ref[rows, 256 * h : 256 * h + 128], rope_rows], axis=1)
            sc = lax.dot_general(qcat[h], kcat, (((1,), (1,)), ((), ())), preferred_element_type=F32)
            sc = jnp.where(seen, sc * scale, -1e30)
            new = jnp.max(sc, axis=1, keepdims=True)
            if g:
                old = m_ref[h]
                new = jnp.maximum(old, new)
                fade = jnp.exp2(old - new)
            w = jnp.exp2(sc - new)
            mass = jnp.sum(w, axis=1, keepdims=True)
            mix = jnp.dot(w.astype(BF16), up_ref[rows, 256 * h + 128 : 256 * h + 256], preferred_element_type=F32)
            if g:
                mass += l_ref[h] * fade
                mix += acc_ref[h] * fade
            if g + many < 8:
                m_ref[h] = new
                l_ref[h] = mass
                acc_ref[h] = mix
            else:
                out_ref[:, VDIM * h : VDIM * (h + 1)] = (mix / mass).astype(BF16)

    sequence = [(0, 0)]

    def k_step(*steps):
        for step in steps:
            for g in gk:
                if isinstance(step, int):
                    g.arrive1(step)
                else:
                    g.arrive2(*step)
            sequence.append((step, 0) if isinstance(step, int) else step)

    def q_step(*steps):
        for step in steps:
            for g in gq:
                if isinstance(step, int):
                    g.arrive1(step)
                else:
                    g.arrive2(*step)

    q_step(2, 1)
    q_step((0, 2), (0, 1))
    k_step(2, 1)
    q_step(3)
    loads[5].wait()
    expand(0)
    k_step((0, 2), (0, 1), 3)
    q_step((2, 2), (2, 1), (1, 2), (1, 1), (0, 3))
    expand(1)
    expand(2)
    k_step((2, 2), (2, 1), (1, 2), (1, 1))
    q_step((3, 2), (3, 1), (2, 3), (1, 3))
    expand(3)
    k_step((0, 3), (3, 2), (3, 1))
    q_step((3, 3))
    loads[4].wait()
    queries()
    attend(0, 2)
    expand(4)
    attend(2, 2)
    k_step((2, 3), (1, 3), (3, 3))
    expand(5)
    attend(4, 2)
    expand(6)
    expand(7)
    attend(6, 2)

    for copy in sent:
        copy.wait_send()
    assert count[0] <= SEMS, count[0]


SEMS = 176
FREQ = np.zeros((1, 128), np.float32)
FREQ[0, :64] = np.tile(
    np.float32(10000.0) ** (-(np.arange(32, dtype=np.float32) * np.float32(2.0) / np.float32(64))), 2
)


def body(tokens, positions, w_down_q, w_down_kv, w_rope_key, gain_query, gain_kv, w_up_q, w_up_kv):
    vmem = pl.BlockSpec(memory_space=pltpu.VMEM)
    smem = pl.BlockSpec(memory_space=pltpu.SMEM)
    any_ = pl.BlockSpec(memory_space=pl.ANY)

    def sums(lead, cuts):
        out = []
        for (_, aw), (_, bw) in cuts:
            out.append([pltpu.VMEM(lead + (w,), F32) for w in (aw, bw, aw, bw, aw, bw)])
        return out

    def mids(cuts):
        return [pltpu.VMEM((4, RUN, a[1] + b[1]), F32) for a, b in cuts]

    tokens, w_rope_key = tokens.T, w_rope_key.T
    scratch = (
        [pltpu.VMEM(a.shape, a.dtype) for a in (tokens, w_down_q, w_down_kv, w_rope_key, w_up_q, w_up_kv)]
        + [pltpu.VMEM((1, 128), F32), pltpu.VMEM((QL // 128, 128), F32), pltpu.VMEM((1, KVL), F32)]
        + [pltpu.VMEM((4, 4, RUN, QL), F32), pltpu.VMEM((4, 4, RUN, LINE), F32)]
        + [sums((4, RUN), CUTS_Q), sums((4, RUN), CUTS_K), mids(CUTS_Q), mids(CUTS_K)]
        + [sums((RUN,), CUTS_Q), sums((RUN,), CUTS_K)]
        + [
            pltpu.VMEM((RUN, QL), F32),
            pltpu.VMEM((RUN, LINE), F32),
            pltpu.VMEM((16, RUN, QL), BF16),
            pltpu.VMEM((2, 16, 2, 4, RUN, LINE), BF16),
            pltpu.VMEM((8 * GROUP, 1024), BF16),
            pltpu.VMEM((8 * GROUP, 128), BF16),
            pltpu.VMEM((HEAD_DEV, 256, 256), BF16),
            pltpu.VMEM((HEAD_DEV, 256, 1), F32),
            pltpu.VMEM((HEAD_DEV, 256, 1), F32),
            pltpu.VMEM((HEAD_DEV, 256, VDIM), F32),
            pltpu.SemaphoreType.DMA((9,)),
            pltpu.SemaphoreType.DMA((SEMS,)),
            pltpu.SemaphoreType.DMA((SEMS,)),
            pltpu.SemaphoreType.REGULAR((3, 2)),
        ]
    )
    return pl.pallas_call(
        kernel,
        out_shape=jax.ShapeDtypeStruct((256, HEAD_DEV * VDIM), BF16),
        in_specs=[smem] + [any_] * 9,
        out_specs=vmem,
        scratch_shapes=scratch,
        compiler_params=pltpu.CompilerParams(
            collective_id=0, has_side_effects=True, vmem_limit_bytes=56 * 1024 * 1024
        ),
    )(
        positions, jnp.asarray(FREQ), gain_query.reshape(QL // 128, 128), gain_kv.reshape(1, KVL),
        tokens, w_down_q, w_down_kv, w_rope_key, w_up_q, w_up_kv,
    )


def solution(mesh):
    in_specs = (
        P("seq", "tensor"),
        P("seq"),
        P("tensor", None),
        P("tensor", None),
        P("tensor", None),
        P(),
        P(),
        P(None, "tensor"),
        P(None, "tensor"),
    )
    out_specs = P("seq", "tensor")
    return jax.shard_map(body, mesh=mesh, in_specs=in_specs, out_specs=out_specs, check_vma=False)
```
